32 devices in a mesh: cluster: 8 (over y, x, core), matrix: 4 (over z).
Axes of the slice: x: 2, y: 2, z: 4, core: 2. Of those that a mesh axis runs over, the one named last changes fastest.
Arguments:
- matrix_pressure_iterate: float32 [32768, 128], P(('cluster', 'matrix')), may hold values from 0 to 2
- matrix_water_saturation: float32 [32768, 128], P(('cluster', 'matrix')), may hold values from 0.05 to 0.95
- matrix_pressure_prior: float32 [32768, 128], P(('cluster', 'matrix')), may hold values from 0 to 2
- matrix_saturation_prior: float32 [32768, 128], P(('cluster', 'matrix')), may hold values from 0.05 to 0.95
- matrix_pore_volume: float32 [32768, 128], P(('cluster', 'matrix')), may hold values from 0.5 to 5
- cell_shape_factor: float32 [32768, 128], P(('cluster', 'matrix')), may hold values from 0.2 to 5
- fracture_pressure: float32 [1024, 128], P(('cluster', 'matrix')), may hold values from 0 to 2
- fracture_saturation: float32 [1024, 128], P(('cluster', 'matrix')), may hold values from 0.05 to 0.95
- fracture_pressure_old: float32 [1024, 128], P(('cluster', 'matrix')), may hold values from 0 to 2
- fracture_saturation_old: float32 [1024, 128], P(('cluster', 'matrix')), may hold values from 0.05 to 0.95
- fracture_pore: float32 [1024, 128], P(('cluster', 'matrix')), may hold values from 0.05 to 0.5
- fracture_trans: float32 [1024, 128], P(('cluster', 'matrix')), may hold values from 0.5 to 10
- feeding_owner_group: int32 [32768, 1], P(('cluster', 'matrix')), may hold values from 0 to 7; in each aligned block of 1024 rows (0 to 1023, 1024 to 2047, ...) at most 256 rows name the same one
- owner_tile_position: int32 [32768], P(('cluster', 'matrix')), may hold values from 0 to 127
Outputs:
- matrix_residual: float32 [2, 32768, 128], P(None, ('cluster', 'matrix'))
- fracture_residual: float32 [2, 1024, 128], P(None, ('cluster', 'matrix'))
- jacobian: float32 [4, 32768, 128], P(None, ('cluster', 'matrix'))
The draws below stay inside these ranges and needn't reach their ends.
Inputs may be any that keep to these rules, and one draw needn't show every extreme that they name: `feeding_owner_group`: among the rows of one device, each owner group is named by at most 256 rows, a bound that some block reaches.
All inputs are finite; a program needn't handle non-finite values. Where the reference program divides by a largest or mean magnitude, that divisor is 1e-20 or more.
Results may differ from the reference program's by a relative error of at most 0.0003.
Values sent between devices are 32-bit elements; how exact they have to be, the bound alone decides.
No kernel may reach another device: no remote copies, remote signals or barrier semaphores. Data moves between devices by JAX's collectives and lax.ppermute only.
A program may use at most 64 MiB of HBM per device.

```python
import math
import jax
import jax.numpy as jnp
import numpy as np

TILE_CELL_COUNT = 128
MATRIX_PER_UNIT = 1024
FRACTURE_PER_UNIT = 32
OWNER_SLOT_LIMIT = 256
MATRIX_TILE_TOTAL = 32768
FTILES = 1024
N_CLUSTER = 8
N_MATRIX = 4


def set_ends(drawn, rng, smallest, high):
    place = [jax.random.randint(jax.random.fold_in(rng, axis), (), 0, length) for axis, length in enumerate(drawn.shape)]
    widest = drawn.shape.index(max(drawn.shape))
    beside = place[:widest] + [(place[widest] + 1) % drawn.shape[widest]] + place[widest + 1:]
    return drawn.at[tuple(place)].set(smallest).at[tuple(beside)].set(high)


def block_levels(rng, shape, pieces, least, top_value):
    level, own = 1.0, jax.random.fold_in(rng, 6)
    for position, shards_of in pieces:
        steps = jnp.exp(jax.random.uniform(jax.random.fold_in(own, position), (shards_of,), jnp.float32, least / len(pieces), top_value / len(pieces)))
        level = level * jnp.repeat(steps, shape[position] // shards_of).reshape([-1 if axis == position else 1 for axis in range(len(shape))])
    return level


def shared_out(key, own, number, rows, count, top, bound, skew):
    order = jax.random.permutation(key, count)
    crowded, usual = load_shares(count, rows * top, bound, skew, True), load_shares(count, rows * top, bound, skew, False)
    places = jnp.arange(count)

    def named(sizes, offset_by):
        used = int((sizes > 0).sum())
        fixed = max(1, used // 4)
        shifted = fixed + (places - fixed + offset_by * (used - fixed)) % max(1, count - fixed)
        return jnp.zeros((count,), jnp.int32).at[order[jnp.where(places < fixed, places, shifted)]].set(jnp.asarray(sizes, jnp.int32))

    sizes = jnp.where(number % 4 == 0, named(crowded, number // 4), named(usual, number - number // 4 - 1))
    mixed = jax.random.permutation(jax.random.fold_in(own, 3), count)
    donor, receiver = mixed[0:count // 2 * 2:2], mixed[1:count // 2 * 2:2]
    margin = jnp.minimum(sizes[donor] - 1, bound - sizes[receiver]) // 2
    margin = jnp.where((donor == order[0]) | (receiver == order[0]) | (sizes[receiver] == 0), 0, jnp.maximum(margin, 0))
    shifted = jax.random.randint(jax.random.fold_in(own, 4), (count // 2,), 0, 1 << 20) % (margin + 1)
    sizes = sizes.at[donor].add(-shifted).at[receiver].add(shifted)
    items = jnp.searchsorted(jnp.cumsum(sizes), jnp.arange(rows * top), side="right").astype(jnp.int32)
    grid = items.reshape(top, rows).T
    grid = grid[jax.random.permutation(jax.random.fold_in(own, 1), rows)]
    offset_by = jax.random.randint(jax.random.fold_in(own, 2), (rows, 1), 0, top)
    return jnp.take_along_axis(grid, (jnp.arange(top)[None, :] + offset_by) % top, axis=1)


def load_shares(number_of, total, limit, skew, full):
    portions = [(1 << 20) // math.isqrt(standing ** skew) + 1 for standing in range(1, number_of + 1)]
    largest = limit if full else min(limit, max(-(-total // number_of), total * portions[0] // sum(portions)))
    least = 1 if total - largest >= number_of - 1 else 0
    given, spare = [largest] + [least] * (number_of - 1), total - largest - least * (number_of - 1)
    while spare > 0:
        candidates = [i for i in range(1, number_of) if given[i] < largest] or [i for i in range(1, number_of) if given[i] < limit]
        whole, remaining = sum([portions[i] for i in candidates]), spare
        for i in candidates:
            more = min(limit - given[i], max(1, remaining * portions[i] // whole), spare)
            given[i] = given[i] + more
            spare = spare - more
    return np.array(given)


def setup_inputs(seed: int = 0) -> dict:
    splits = jax.random.split(jax.random.key(seed), 15)
    matrix_pressure_iterate = jnp.clip(2.0 * jax.random.uniform(splits[0], (MATRIX_TILE_TOTAL, TILE_CELL_COUNT), jnp.float32) ** block_levels(splits[0], (MATRIX_TILE_TOTAL, TILE_CELL_COUNT), ((0, 32),), -0.2, 0.2), 0.0, 2.0)
    matrix_water_saturation = jnp.clip(0.05 + 0.9 * jax.random.uniform(splits[1], (MATRIX_TILE_TOTAL, TILE_CELL_COUNT), jnp.float32) ** block_levels(splits[1], (MATRIX_TILE_TOTAL, TILE_CELL_COUNT), ((0, 32),), -0.2, 0.2), 0.05, 0.95)
    matrix_pressure_prior = jnp.clip(2.0 * jax.random.uniform(splits[2], (MATRIX_TILE_TOTAL, TILE_CELL_COUNT), jnp.float32) ** block_levels(splits[2], (MATRIX_TILE_TOTAL, TILE_CELL_COUNT), ((0, 32),), -0.2, 0.2), 0.0, 2.0)
    matrix_saturation_prior = jnp.clip(0.05 + 0.9 * jax.random.uniform(splits[3], (MATRIX_TILE_TOTAL, TILE_CELL_COUNT), jnp.float32) ** block_levels(splits[3], (MATRIX_TILE_TOTAL, TILE_CELL_COUNT), ((0, 32),), -0.2, 0.2), 0.05, 0.95)
    matrix_pore_volume = jnp.clip(jnp.exp(math.log(5.0) - 2.3025851 * jax.random.uniform(splits[4], (MATRIX_TILE_TOTAL, TILE_CELL_COUNT), jnp.float32) ** block_levels(splits[4], (MATRIX_TILE_TOTAL, TILE_CELL_COUNT), ((0, 32),), -0.2, 0.2)), 0.5, 5.0)
    cell_shape_factor = jnp.clip(jnp.exp(math.log(5.0) - 3.218876 * jax.random.uniform(splits[5], (MATRIX_TILE_TOTAL, TILE_CELL_COUNT), jnp.float32) ** block_levels(splits[5], (MATRIX_TILE_TOTAL, TILE_CELL_COUNT), ((0, 32),), -0.2, 0.2)), 0.2, 5.0)
    fracture_pressure = jnp.clip(2.0 * jax.random.uniform(splits[6], (FTILES, TILE_CELL_COUNT), jnp.float32) ** block_levels(splits[6], (FTILES, TILE_CELL_COUNT), ((0, 32),), -0.2, 0.2), 0.0, 2.0)
    fracture_saturation = jnp.clip(0.05 + 0.9 * jax.random.uniform(splits[7], (FTILES, TILE_CELL_COUNT), jnp.float32) ** block_levels(splits[7], (FTILES, TILE_CELL_COUNT), ((0, 32),), -0.2, 0.2), 0.05, 0.95)
    fracture_pressure_old = jnp.clip(2.0 * jax.random.uniform(splits[8], (FTILES, TILE_CELL_COUNT), jnp.float32) ** block_levels(splits[8], (FTILES, TILE_CELL_COUNT), ((0, 32),), -0.2, 0.2), 0.0, 2.0)
    fracture_saturation_old = jnp.clip(0.05 + 0.9 * jax.random.uniform(splits[9], (FTILES, TILE_CELL_COUNT), jnp.float32) ** block_levels(splits[9], (FTILES, TILE_CELL_COUNT), ((0, 32),), -0.2, 0.2), 0.05, 0.95)
    fracture_pore = jnp.clip(jnp.exp(math.log(0.5) - 2.3025851 * jax.random.uniform(splits[10], (FTILES, TILE_CELL_COUNT), jnp.float32) ** block_levels(splits[10], (FTILES, TILE_CELL_COUNT), ((0, 32),), -0.2, 0.2)), 0.05, 0.5)
    fracture_trans = jnp.clip(jnp.exp(math.log(10.0) - 2.9957323 * jax.random.uniform(splits[11], (FTILES, TILE_CELL_COUNT), jnp.float32) ** block_levels(splits[11], (FTILES, TILE_CELL_COUNT), ((0, 32),), -0.2, 0.2)), 0.5, 10.0)
    feeding_owner_group_keys = jax.random.split(jax.random.fold_in(splits[12], 1), MATRIX_TILE_TOTAL // MATRIX_PER_UNIT)
    feeding_owner_group_turns = jax.random.permutation(jax.random.fold_in(splits[12], 3), MATRIX_TILE_TOTAL // MATRIX_PER_UNIT)
    feeding_owner_group = jax.vmap(lambda own, number: shared_out(jax.random.fold_in(splits[12], 2), own, number, MATRIX_PER_UNIT, N_CLUSTER, 1, OWNER_SLOT_LIMIT, 1))(feeding_owner_group_keys, feeding_owner_group_turns).reshape((MATRIX_TILE_TOTAL, 1))
    owner_tile_position = set_ends(jax.random.randint(splits[13], (MATRIX_TILE_TOTAL,), 0, FRACTURE_PER_UNIT * N_MATRIX), jax.random.fold_in(splits[13], 1), 0, (FRACTURE_PER_UNIT * N_MATRIX) - 1).astype(jnp.int32)
    return dict(matrix_pressure_iterate=matrix_pressure_iterate, matrix_water_saturation=matrix_water_saturation, matrix_pressure_prior=matrix_pressure_prior, matrix_saturation_prior=matrix_saturation_prior, matrix_pore_volume=matrix_pore_volume, cell_shape_factor=cell_shape_factor, fracture_pressure=fracture_pressure, fracture_saturation=fracture_saturation, fracture_pressure_old=fracture_pressure_old, fracture_saturation_old=fracture_saturation_old, fracture_pore=fracture_pore, fracture_trans=fracture_trans, feeding_owner_group=feeding_owner_group, owner_tile_position=owner_tile_position)


VISC_WATER = 1.0
VISC_OIL = 3.0
ROCK_COMPRESS = 0.1
EPSILON = 1e-6


def mobility(saturation):
    return saturation * saturation / VISC_WATER, (1.0 - saturation) * (1.0 - saturation) / VISC_OIL


def storage(pressure, saturation, pressure_old, saturation_old, pore):
    factor = 1.0 + ROCK_COMPRESS * pressure
    factor_old = 1.0 + ROCK_COMPRESS * pressure_old
    water = pore * (factor * saturation - factor_old * saturation_old)
    oil = pore * (factor * (1.0 - saturation) - factor_old * (1.0 - saturation_old))
    return water, oil, factor


def chain_flow(pressure, saturation, trans):
    drop = pressure[:, :-1] - pressure[:, 1:]
    upwind = jnp.where(drop >= 0.0, saturation[:, :-1], saturation[:, 1:])
    water_mob, oil_mob = mobility(upwind)
    links = trans[:, :-1]
    water = links * water_mob * drop
    oil = links * oil_mob * drop

    def net_flow(flow):
        return jnp.pad(flow, ((0, 0), (0, 1))) - jnp.pad(flow, ((0, 0), (1, 0)))

    return net_flow(water), net_flow(oil)


def reference(matrix_pressure_iterate, matrix_water_saturation, matrix_pressure_prior, matrix_saturation_prior, matrix_pore_volume, cell_shape_factor, fracture_pressure, fracture_saturation, fracture_pressure_old, fracture_saturation_old, fracture_pore, fracture_trans, feeding_owner_group, owner_tile_position):
    owner = (feeding_owner_group[:, 0] * (FRACTURE_PER_UNIT * N_MATRIX) + owner_tile_position).astype(jnp.int32)
    other_pressure = jnp.take(fracture_pressure, owner, axis=0)
    other_saturation = jnp.take(fracture_saturation, owner, axis=0)
    store_water, store_oil, factor = storage(matrix_pressure_iterate, matrix_water_saturation, matrix_pressure_prior, matrix_saturation_prior, matrix_pore_volume)
    drop = matrix_pressure_iterate - other_pressure
    upstream = drop >= 0.0
    upwind = jnp.where(upstream, matrix_water_saturation, other_saturation)
    water_mob, oil_mob = mobility(upwind)
    water_flow = cell_shape_factor * water_mob * drop
    oil_flow = cell_shape_factor * oil_mob * drop
    matrix_water = store_water + water_flow
    matrix_oil = store_oil + oil_flow
    jac_wp = matrix_pore_volume * ROCK_COMPRESS * matrix_water_saturation + cell_shape_factor * water_mob
    jac_ws = matrix_pore_volume * factor + jnp.where(upstream, cell_shape_factor * 2.0 * matrix_water_saturation / VISC_WATER * drop, 0.0)
    jac_op = matrix_pore_volume * ROCK_COMPRESS * (1.0 - matrix_water_saturation) + cell_shape_factor * oil_mob
    jac_os = -matrix_pore_volume * factor + jnp.where(upstream, -cell_shape_factor * 2.0 * (1.0 - matrix_water_saturation) / VISC_OIL * drop, 0.0)
    water_sum = jax.ops.segment_sum(water_flow, owner, num_segments=FTILES)
    oil_sum = jax.ops.segment_sum(oil_flow, owner, num_segments=FTILES)
    frac_water, frac_oil, frac_factor = storage(fracture_pressure, fracture_saturation, fracture_pressure_old, fracture_saturation_old, fracture_pore)
    net_water, net_oil = chain_flow(fracture_pressure, fracture_saturation, fracture_trans)
    fracture_water = frac_water + net_water - water_sum
    fracture_oil = frac_oil + net_oil - oil_sum
    top_water = jnp.maximum(jnp.max(jnp.abs(matrix_water)), jnp.max(jnp.abs(fracture_water)))
    top_oil = jnp.maximum(jnp.max(jnp.abs(matrix_oil)), jnp.max(jnp.abs(fracture_oil)))
    matrix_residual = jnp.stack([matrix_water / (top_water + EPSILON), matrix_oil / (top_oil + EPSILON)])
    fracture_residual = jnp.stack([fracture_water / (top_water + EPSILON), fracture_oil / (top_oil + EPSILON)])
    jacobian = jnp.stack([jac_wp, jac_ws, jac_op, jac_os])
    return matrix_residual, fracture_residual, jacobian
```

```python
import functools

import jax
import jax.numpy as jnp
from jax import lax
from jax.experimental import pallas as pl
from jax.experimental.pallas import tpu as pltpu
from jax.sharding import PartitionSpec as P

VISC_WATER = 1.0
VISC_OIL = 3.0
ROCK_COMPRESS = 0.1
EPSILON = 1e-06
LIFT = 2.0**64
VMEM = pl.BlockSpec(memory_space=pltpu.VMEM)
SMEM = pl.BlockSpec(memory_space=pltpu.SMEM)
F32 = jnp.float32
BF16 = jnp.bfloat16


def params(mib):
    return pltpu.CompilerParams(vmem_limit_bytes=mib << 20)


def struct(*shape, dtype=F32):
    return jax.ShapeDtypeStruct(shape, dtype)


def mobility(saturation):
    return (
        saturation * saturation / VISC_WATER,
        (1.0 - saturation) * (1.0 - saturation) / VISC_OIL,
    )


def storage(pressure, saturation, pressure_old, saturation_old, pore):
    factor = 1.0 + ROCK_COMPRESS * pressure
    factor_old = 1.0 + ROCK_COMPRESS * pressure_old
    water = pore * (factor * saturation - factor_old * saturation_old)
    oil = pore * (factor * (1.0 - saturation) - factor_old * (1.0 - saturation_old))
    return (water, oil, factor)


def split(x, parts):
    terms = []
    for _ in range(parts - 1):
        term = x.astype(BF16)
        terms.append(term)
        x = x - term.astype(F32)
    terms.append(x.astype(BF16))
    return terms


def exchange_kernel(
    sizes, dev, group, position, pressure, saturation, shape_factor, mine, other,
    drop_out, upwind_out, own_sums, other_sums, state, picks, terms,
):
    members, tiles, rows, width = sizes
    half = mine.shape[0]
    total = 2 * half
    group_tiles = members * tiles
    relative = group[...] ^ (dev[0] // members)
    index = (
        (relative & 1) * half
        + (relative >> 1) * group_tiles
        + (position[...] ^ ((dev[0] % members) * tiles))
    )
    step = min(256, half)
    for source, base in ((mine, 0), (other, half)):
        for start in range(0, half, step):
            for lane, lift in ((0, LIFT), (width, 1.0)):
                values = source[start : start + step, lane : lane + width] * lift
                for k, term in enumerate(split(values, 3)):
                    column = (3 if lane else 0) * width + k * width
                    state[base + start : base + start + step, column : column + width] = term
    lanes = lax.broadcasted_iota(jnp.int32, (128, 128), 1)
    block = 256
    for start in range(0, rows, block):
        for sub in range(0, block, 128):
            spread = jnp.broadcast_to(index[:, start + sub : start + sub + 128], (128, 128)).T
            for column in range(0, total, 128):
                picks[sub : sub + 128, column : column + 128] = jnp.where(
                    spread == lanes + column, 1.0, 0.0
                ).astype(BF16)
        found = jnp.dot(picks[...], state[...], preferred_element_type=F32)
        here = slice(start, start + block)
        other_pressure = (
            (found[:, :width] + found[:, width : 2 * width]) + found[:, 2 * width : 3 * width]
        ) * (1.0 / LIFT)
        other_saturation = (
            found[:, 3 * width : 4 * width] + found[:, 4 * width : 5 * width]
        ) + found[:, 5 * width :]
        drop = pressure[here, :] - other_pressure
        upwind = jnp.where(drop >= 0.0, saturation[here, :], other_saturation)
        water_mob, oil_mob = mobility(upwind)
        factor = shape_factor[here, :] * drop
        drop_out[here, :] = drop
        upwind_out[here, :] = upwind
        for k, flow in enumerate((factor * water_mob, factor * oil_mob)):
            high, low = split(flow, 2)
            terms[here, 2 * k * width : (2 * k + 1) * width] = high
            terms[here, (2 * k + 1) * width : (2 * k + 2) * width] = low
    sublanes = lax.broadcasted_iota(jnp.int32, (step, rows), 0)
    for target, base in ((other_sums, half), (own_sums, 0)):
        for start in range(0, half, step):
            owned = jnp.where(index == sublanes + (base + start), 1.0, 0.0).astype(BF16)
            sums = jnp.dot(owned, terms[...], preferred_element_type=F32)
            target[start : start + step, :width] = sums[:, :width] + sums[:, width : 2 * width]
            target[start : start + step, width:] = (
                sums[:, 2 * width : 3 * width] + sums[:, 3 * width :]
            )


def matrix_kernel(
    pressure, saturation, pressure_old, saturation_old, pore, shape_factor, drop_in, upwind_in,
    residual, jacobian, top,
):
    drop = drop_in[...]
    sat = saturation[...]
    vol = pore[...]
    csf = shape_factor[...]
    store_water, store_oil, factor = storage(
        pressure[...], sat, pressure_old[...], saturation_old[...], vol
    )
    water_mob, oil_mob = mobility(upwind_in[...])
    upstream = drop >= 0.0
    water = store_water + csf * water_mob * drop
    oil = store_oil + csf * oil_mob * drop
    residual[0] = water
    residual[1] = oil
    jacobian[0] = vol * ROCK_COMPRESS * sat + csf * water_mob
    jacobian[1] = vol * factor + jnp.where(upstream, csf * 2.0 * sat / VISC_WATER * drop, 0.0)
    jacobian[2] = vol * ROCK_COMPRESS * (1.0 - sat) + csf * oil_mob
    jacobian[3] = -vol * factor + jnp.where(
        upstream, -csf * 2.0 * (1.0 - sat) / VISC_OIL * drop, 0.0
    )

    @pl.when(pl.program_id(0) == 0)
    def _():
        top[...] = jnp.zeros_like(top)

    for k, values in enumerate((water, oil)):
        largest = jnp.max(jnp.abs(values), axis=0, keepdims=True)
        top[k : k + 1, :] = jnp.maximum(top[k : k + 1, :], largest)


def fracture_kernel(
    pressure, saturation, pressure_old, saturation_old, pore, trans, matrix_top, *rest
):
    pieces, (residual, tops) = rest[:-2], rest[-2:]
    width = pressure.shape[1]
    p, s = pressure[...], saturation[...]
    water, oil, _ = storage(p, s, pressure_old[...], saturation_old[...], pore[...])
    lane = lax.broadcasted_iota(jnp.int32, p.shape, 1)
    drop = p - pltpu.roll(p, width - 1, 1)
    upwind = jnp.where(drop >= 0.0, s, pltpu.roll(s, width - 1, 1))
    sums = pieces[0][...]
    for piece in pieces[1:]:
        sums = sums + piece[...]
    for k, (stored, mob) in enumerate(zip((water, oil), mobility(upwind))):
        link = jnp.where(lane < width - 1, trans[...] * mob * drop, 0.0)
        net = link - jnp.where(lane > 0, pltpu.roll(link, 1, 1), 0.0)
        values = stored + net - sums[:, k * width : (k + 1) * width]
        residual[k] = values
        largest = jnp.max(jnp.abs(values), axis=0, keepdims=True)
        largest = jnp.maximum(largest, matrix_top[k : k + 1, :])
        tops[:, k : k + 1, :] = jnp.broadcast_to(largest[None], (tops.shape[0], 1, width))


def scale_kernel(tops, matrix, fracture, matrix_out, fracture_out):
    for k in range(2):
        scale = 1.0 / (jnp.max(tops[:, k, :], keepdims=True) + EPSILON)
        matrix_out[k] = matrix[k] * scale
        fracture_out[k] = fracture[k] * scale


def per_device(
    matrix_pressure_iterate,
    matrix_water_saturation,
    matrix_pressure_prior,
    matrix_saturation_prior,
    matrix_pore_volume,
    cell_shape_factor,
    fracture_pressure,
    fracture_saturation,
    fracture_pressure_old,
    fracture_saturation_old,
    fracture_pore,
    fracture_trans,
    feeding_owner_group,
    owner_tile_position,
):
    groups = lax.axis_size("cluster")
    members = lax.axis_size("matrix")
    rows, width = matrix_pressure_iterate.shape
    tiles = fracture_pressure.shape[0]
    group_tiles = members * tiles
    chips = groups // 2
    half = chips * group_tiles
    dev = (lax.axis_index("cluster") * members + lax.axis_index("matrix")).reshape(1)

    def swap(x, axis, bits):
        return lax.ppermute(x, axis, [(i, i ^ bits) for i in range(lax.axis_size(axis))])

    own = jnp.concatenate([fracture_pressure, fracture_saturation], axis=1)
    layer = jnp.concatenate([own] + [swap(own, "matrix", z) for z in range(1, members)], axis=0)
    mine = jnp.concatenate([layer] + [swap(layer, "cluster", 2 * c) for c in range(1, chips)], axis=0)
    other = swap(mine, "cluster", 1)
    drop, upwind, own_sums, other_sums = pl.pallas_call(
        functools.partial(exchange_kernel, (members, tiles, rows, width)),
        in_specs=[SMEM] + [VMEM] * 7,
        out_specs=[VMEM] * 4,
        out_shape=[struct(rows, width)] * 2 + [struct(half, 2 * width)] * 2,
        scratch_shapes=[
            pltpu.VMEM((2 * half, 6 * width), BF16),
            pltpu.VMEM((256, 2 * half), BF16),
            pltpu.VMEM((rows, 4 * width), BF16),
        ],
        compiler_params=params(24 if half <= 1024 else 60),
        name="exchange",
    )(
        dev,
        feeding_owner_group.reshape(1, rows),
        owner_tile_position.reshape(1, rows),
        matrix_pressure_iterate,
        matrix_water_saturation,
        cell_shape_factor,
        mine,
        other,
    )
    block = pl.BlockSpec((256, width), lambda i: (i, 0))
    residual, jacobian, matrix_top = pl.pallas_call(
        matrix_kernel,
        grid=(rows // 256,),
        in_specs=[block] * 8,
        out_specs=[
            pl.BlockSpec((2, 256, width), lambda i: (0, i, 0)),
            pl.BlockSpec((4, 256, width), lambda i: (0, i, 0)),
            pl.BlockSpec((2, width), lambda i: (0, 0)),
        ],
        out_shape=[struct(2, rows, width), struct(4, rows, width), struct(2, width)],
        compiler_params=params(24),
        cost_estimate=pl.CostEstimate(
            flops=40 * rows * width, bytes_accessed=56 * rows * width, transcendentals=0
        ),
        name="matrix",
    )(
        matrix_pressure_iterate,
        matrix_water_saturation,
        matrix_pressure_prior,
        matrix_saturation_prior,
        matrix_pore_volume,
        cell_shape_factor,
        drop,
        upwind,
    )
    chip_sums = own_sums + swap(other_sums, "cluster", 1)
    part = [chip_sums[c * group_tiles : (c + 1) * group_tiles] for c in range(chips)]
    layer_sums = part[0]
    for c in range(1, chips):
        layer_sums = layer_sums + swap(part[c], "cluster", 2 * c)
    part = [layer_sums[z * tiles : (z + 1) * tiles] for z in range(members)]
    pieces = [part[0]] + [swap(part[z], "matrix", z) for z in range(1, members)]
    fracture, tops = pl.pallas_call(
        fracture_kernel,
        in_specs=[VMEM] * (7 + members),
        out_specs=[VMEM] * 2,
        out_shape=[struct(2, tiles, width), struct(groups * members, 2, width)],
        compiler_params=params(8),
        name="fracture",
    )(
        fracture_pressure,
        fracture_saturation,
        fracture_pressure_old,
        fracture_saturation_old,
        fracture_pore,
        fracture_trans,
        matrix_top,
        *pieces,
    )
    tops = lax.all_to_all(tops, ("cluster", "matrix"), split_axis=0, concat_axis=0, tiled=True)
    matrix_residual, fracture_residual = pl.pallas_call(
        scale_kernel,
        in_specs=[VMEM] * 3,
        out_specs=[VMEM] * 2,
        out_shape=[struct(2, rows, width), struct(2, tiles, width)],
        compiler_params=params(8),
        name="scale",
    )(tops, residual, fracture)
    return (matrix_residual, fracture_residual, jacobian)


def solution(mesh):
    rows = P(("cluster", "matrix"), None)
    stacked = P(None, ("cluster", "matrix"), None)
    return jax.shard_map(
        per_device,
        mesh=mesh,
        in_specs=(rows,) * 13 + (P(("cluster", "matrix")),),
        out_specs=(stacked,) * 3,
        check_vma=False,
    )
```
